32 devices in a mesh: row: 8 (over z, y), col: 4 (over x, core).
Axes of the slice: x: 2, y: 2, z: 4, core: 2. Of those that a mesh axis runs over, the one named last changes fastest.
Arguments:
- trailing: bfloat16 [12288, 12288], P('row', 'col'), may hold values from -6 to 6
- rows_a: int32 [8, 12], replicated, may hold values from 0 to 11, as said below
- counts_a: int32 [8], replicated, may hold values from 1 to 12, as said below
- factor_a: bfloat16 [12288, 512], P('row'), may hold values from -0.0546875 to 0.0546875
- rows_b: int32 [8, 12], replicated, may hold values from 0 to 11, as said below
- counts_b: int32 [8], replicated, may hold values from 1 to 12, as said below
- factor_b: bfloat16 [12288, 512], P('row'), may hold values from -0.0546875 to 0.0546875
- factor_top: bfloat16 [512, 512], replicated, may hold values from -0.25 to 0.25
- base_a: float32 [512, 512], P('col'), may hold values from -3 to 3
- base_b: float32 [512, 512], P('col'), may hold values from -3 to 3
Outputs:
- column_a: bfloat16 [12288, 512], P('row')
- diag_a: float32 [512, 512], P('col')
- column_b: bfloat16 [12288, 512], P('row')
- top_b: bfloat16 [512, 512], P('col')
- diag_b: float32 [512, 512], P('col')
The draws below stay inside these ranges and needn't reach their ends.
Inputs may be any that keep to these rules, and one draw needn't show every extreme that they name: `rows_a`: the first counts_a[r] entries of row r are distinct; the rest of the row is padding. `counts_a`: some owner uses all 12 slots in every draw. `rows_b`: the first counts_b[r] entries of row r are distinct and lie among the first counts_a[r] entries of row r of rows_a; the rest is padding. counts_b[r] <= counts_a[r]; some owner uses all 12 slots in every draw.
All inputs are finite; a program needn't handle non-finite values.
Results may differ from the reference program's by a relative error of at most 0.007.
Values may be sent and summed in bfloat16 or wider, within the bound.
A program may use at most 128 MiB of HBM per device.

```python
import jax
import jax.numpy as jnp
from jax import lax

BS = 128
W = 512
RBD = 12
PAD = 12
OWNERS = 8
COL_OWNERS = 4
CBD = 24
TRAIL = 12288
SROWS = 12288


def structure(key):
    seeded = jax.random.fold_in(key, 11)
    perm_keys = jax.random.split(jax.random.fold_in(seeded, 1), OWNERS)
    orders = jax.vmap(lambda single: jax.random.permutation(single, RBD))(perm_keys).astype(jnp.int32)
    rows_first = orders[:, :PAD]
    counts = jax.random.randint(jax.random.fold_in(seeded, 2), (OWNERS,), PAD // 2, PAD + 1, dtype=jnp.int32)
    busiest = jax.random.randint(jax.random.fold_in(seeded, 3), (), 0, OWNERS, dtype=jnp.int32)
    lighter = (busiest + 1) % OWNERS
    owners = jnp.arange(OWNERS, dtype=jnp.int32)
    counts_first = jnp.where((owners == busiest) | (owners == lighter), PAD, counts).astype(jnp.int32)
    second = jax.random.randint(jax.random.fold_in(seeded, 4), (OWNERS,), (counts_first + 1) // 2, counts_first + 1, dtype=jnp.int32)
    counts_second = jnp.where(owners == busiest, PAD, second)
    counts_second = jnp.where(owners == lighter, PAD - 1, counts_second).astype(jnp.int32)
    shuffle_keys = jax.random.split(jax.random.fold_in(seeded, 5), OWNERS)
    shuffles = jax.vmap(lambda single: jax.random.permutation(single, PAD))(shuffle_keys).astype(jnp.int32)
    slot_ids = jnp.arange(PAD, dtype=jnp.int32)
    scores = jnp.where(slot_ids[None, :] < counts_first[:, None], shuffles, shuffles + PAD)
    sort_order = jnp.argsort(scores, axis=1, stable=True)
    rows_second = jnp.take_along_axis(rows_first, sort_order, axis=1).astype(jnp.int32)
    return (rows_first, counts_first, rows_second, counts_second)


def draw_rows_a(key, part):
    return structure(key)[0]


def draw_counts_a(key, part):
    return structure(key)[1]


def draw_rows_b(key, part):
    return structure(key)[2]


def draw_counts_b(key, part):
    return structure(key)[3]


def steps_of(rng, dims, pieces, low, largest):
    level = 1.0
    for axis_at, parts in pieces:
        steps = jax.random.uniform(jax.random.fold_in(jax.random.fold_in(rng, 6), axis_at), (parts,), jnp.float32, low / len(pieces), largest / len(pieces))
        level = level * jnp.repeat(jnp.exp(steps), dims[axis_at] // parts).reshape((-1,) + (1,) * (len(dims) - 1 - axis_at))
    return level


def scatter_about(key, shape, deviation, most, cuts=(), kind=jnp.bfloat16):
    loudness = steps_of(key, shape, cuts, -0.22, 0.18) if cuts else 1.0
    drawn = jax.random.normal(key, shape, jnp.float32) * deviation * loudness
    return jnp.minimum(jnp.maximum(drawn, -most), most).astype(kind)


def setup_inputs(seed: int = 0) -> dict:
    keys = jax.random.split(jax.random.key(seed), 11)
    trailing = scatter_about(keys[0], (TRAIL, TRAIL), 1.0, 6.0, ((0, 8), (1, 4)))
    rows_a = draw_rows_a(jax.random.fold_in(keys[10], 71), 0)
    counts_a = draw_counts_a(jax.random.fold_in(keys[10], 71), 0)
    factor_a = scatter_about(keys[3], (SROWS, W), SROWS ** -0.5, 0.0546875, ((0, 8),))
    rows_b = draw_rows_b(jax.random.fold_in(keys[10], 71), 0)
    counts_b = draw_counts_b(jax.random.fold_in(keys[10], 71), 0)
    factor_b = scatter_about(keys[6], (SROWS, W), SROWS ** -0.5, 0.0546875, ((0, 8),))
    factor_top = scatter_about(keys[7], (W, W), W ** -0.5, 0.25)
    base_a = scatter_about(keys[8], (W, W), 0.5, 3.0, ((0, 4),), jnp.float32)
    base_b = scatter_about(keys[9], (W, W), 0.5, 3.0, ((0, 4),), jnp.float32)
    return dict(trailing=trailing, rows_a=rows_a, counts_a=counts_a, factor_a=factor_a, rows_b=rows_b, counts_b=counts_b, factor_b=factor_b, factor_top=factor_top, base_a=base_a, base_b=base_b)


def live_mask(counts):
    slot_ids = jnp.arange(PAD, dtype=jnp.int32)
    return (slot_ids[None, :] < counts[:, None]).astype(jnp.float32)


def block_tiles(trailing, rows):
    owners = jnp.arange(OWNERS, dtype=jnp.int32)
    global_ids = rows * OWNERS + owners[:, None]
    row_pos = (owners[:, None] * RBD + rows).reshape(-1).astype(jnp.int32)
    col_pos = ((global_ids % COL_OWNERS) * CBD + global_ids // COL_OWNERS).reshape(-1).astype(jnp.int32)
    blocks = trailing.reshape(TRAIL // BS, BS, TRAIL // BS, BS)
    picked = jnp.take(blocks, row_pos, axis=0)
    picked = jnp.take(picked, col_pos, axis=2)
    slot_count = OWNERS * PAD
    return picked.reshape(slot_count * BS, slot_count * BS)


def reference(trailing, rows_a, counts_a, factor_a, rows_b, counts_b, factor_b, factor_top, base_a, base_b):
    live_a = live_mask(counts_a)
    live_b = live_mask(counts_b)
    gate_a = jnp.repeat(live_a.reshape(-1), BS)[:, None]
    gate_b = jnp.repeat(live_b.reshape(-1), BS)[:, None]
    tiles_a = block_tiles(trailing, rows_a)
    masked_a = factor_a * gate_a.astype(jnp.bfloat16)
    column_a = (-jnp.dot(tiles_a, masked_a, preferred_element_type=jnp.float32) * gate_a).astype(jnp.bfloat16)
    diag_a = base_a - jnp.dot(column_a.T, factor_a, preferred_element_type=jnp.float32)
    pairing = ((rows_b[:, :, None] == rows_a[:, None, :]) & (live_a[:, None, :] > 0.5) & (live_b[:, :, None] > 0.5)).astype(jnp.float32)
    stacked = column_a.reshape(OWNERS, PAD, BS * W).astype(jnp.float32)
    carried = jnp.einsum("rkq,rqx->rkx", pairing, stacked).reshape(SROWS, W).astype(jnp.bfloat16)
    top_b = (-(jnp.dot(carried.T, factor_b, preferred_element_type=jnp.float32) + jnp.dot(diag_a, factor_top.astype(jnp.float32), precision=lax.Precision.HIGHEST))).astype(jnp.bfloat16)
    tiles_b = block_tiles(trailing, rows_b)
    masked_b = factor_b * gate_b.astype(jnp.bfloat16)
    summed_b = jnp.dot(tiles_b, masked_b, preferred_element_type=jnp.float32) + jnp.dot(carried, factor_top, preferred_element_type=jnp.float32)
    column_b = (-summed_b * gate_b).astype(jnp.bfloat16)
    diag_b = base_b - jnp.dot(column_b.T, factor_b, preferred_element_type=jnp.float32) - jnp.dot(top_b.T, factor_top, preferred_element_type=jnp.float32)
    return column_a, diag_a, column_b, top_b, diag_b
```

```python
import functools

import jax
import jax.numpy as jnp
from jax import lax
from jax.experimental import pallas as pl
from jax.experimental.pallas import tpu as pltpu
from jax.sharding import PartitionSpec as P

MESH = pl.DeviceIdType.MESH
CHUNK_SLOTS = 2


def spread_multiply_kernel(
    nz, ny, col_count, fanout, slots, block,
    idx_ref, fa_ref, fb_ref, slab_ref, out_ref,
    held, slab, acc, recv_sem, send_sem, local_sem, slab_sem,
):
    row = lax.axis_index("row")
    col = lax.axis_index("col")
    z = row // ny
    y = row % ny
    chunk = CHUNK_SLOTS * block
    steps = slots // CHUNK_SLOTS
    rows, width = acc.shape[1:]

    def slab_copy(j):
        return pltpu.make_async_copy(
            slab_ref.at[:, pl.ds(pl.multiple_of(j * block, block), block)],
            slab.at[j],
            slab_sem.at[j],
        )

    @pl.loop(0, slab.shape[0])
    def _(j):
        slab_copy(j).start()

    neighbours = (
        (z < nz - 1, row + ny),
        (z > 0, row - ny),
        (y < ny - 1, row + 1),
        (y > 0, row - 1),
    )
    barrier = pltpu.get_barrier_semaphore()
    for there, who in neighbours:
        @pl.when(there)
        def _():
            pl.semaphore_signal(barrier, inc=1, device_id={"row": who}, device_id_type=MESH)
    greeted = (
        jnp.minimum(nz - 1 - z, 1)
        + jnp.minimum(z, 1)
        + jnp.minimum(ny - 1 - y, 1)
        + jnp.minimum(y, 1)
    )
    pl.semaphore_wait(barrier, greeted)

    sources, sends = [], []
    for part in range(fanout):
        owner = col + part * col_count
        oz, oy = owner // ny, owner % ny
        line = y == oy
        sources.append(row == owner)
        sends.append(
            (
                line & (z >= oz) & (z < nz - 1),
                line & (z <= oz) & (z > 0),
                (y >= oy) & (y < ny - 1),
                (y <= oy) & (y > 0),
            )
        )

    for part in range(fanout):
        @pl.when(sources[part])
        def _():
            for node, factor in enumerate((fa_ref, fb_ref)):
                pltpu.make_async_copy(
                    factor, held.at[node, part], local_sem.at[node * fanout + part]
                ).start()
            for node, factor in enumerate((fa_ref, fb_ref)):
                pltpu.make_async_copy(
                    factor, held.at[node, part], local_sem.at[node * fanout + part]
                ).wait()

    def hop(step, part, way):
        node, at = step // steps, step % steps
        piece = held.at[node, part, pl.ds(pl.multiple_of(at * chunk, chunk), chunk)]
        return pltpu.make_async_remote_copy(
            src_ref=piece,
            dst_ref=piece,
            send_sem=send_sem.at[step, part, way],
            recv_sem=recv_sem.at[step, part],
            device_id={"row": neighbours[way][1]},
            device_id_type=MESH,
        )

    acc[...] = jnp.zeros_like(acc)
    tile = 256

    @pl.loop(0, slab.shape[0])
    def _(j):
        slab_copy(j).wait()

    @pl.loop(0, 2 * steps)
    def _(step):
        for part in range(fanout):
            @pl.when(jnp.logical_not(sources[part]))
            def _():
                hop(step, part, 0).wait_recv()
            for way in range(4):
                @pl.when(sends[part][way])
                def _():
                    hop(step, part, way).start()
        node, at = step // steps, step % steps

        @pl.loop(0, rows // tile)
        def _(r):
            here = pl.ds(pl.multiple_of(r * tile, tile), tile)
            total = acc[node, here, :]
            for part in range(fanout):
                left = jnp.concatenate(
                    [
                        slab[idx_ref[node, part, at * CHUNK_SLOTS + k], here, :]
                        for k in range(CHUNK_SLOTS)
                    ],
                    axis=1,
                )
                right = held[node, part, pl.ds(pl.multiple_of(at * chunk, chunk), chunk), :]
                total += jnp.dot(left, right, preferred_element_type=jnp.float32)
            acc[node, here, :] = total

            @pl.when(at == steps - 1)
            def _():
                out_ref[node, here, :] = total.astype(out_ref.dtype)

    @pl.loop(0, 2 * steps)
    def _(step):
        for part in range(fanout):
            for way in range(4):
                @pl.when(sends[part][way])
                def _():
                    hop(step, part, way).wait_send()


def spread_multiply(idx, factor_a, factor_b, trailing, row_count, col_count):
    slots = idx.shape[2]
    rows, width = factor_a.shape
    block = rows // slots
    fanout = row_count // col_count
    ny = max(col_count // 2, 1)
    nz = row_count // ny
    steps = slots // CHUNK_SLOTS
    return pl.pallas_call(
        functools.partial(
            spread_multiply_kernel, nz, ny, col_count, fanout, slots, block
        ),
        out_shape=jax.ShapeDtypeStruct((2, trailing.shape[0], width), jnp.bfloat16),
        in_specs=[
            pl.BlockSpec(memory_space=pltpu.SMEM),
            pl.BlockSpec(memory_space=pl.ANY),
            pl.BlockSpec(memory_space=pl.ANY),
            pl.BlockSpec(memory_space=pl.ANY),
        ],
        out_specs=pl.BlockSpec(memory_space=pltpu.VMEM),
        scratch_shapes=[
            pltpu.VMEM((2, fanout, rows, width), jnp.bfloat16),
            pltpu.VMEM((trailing.shape[1] // block, trailing.shape[0], block), jnp.bfloat16),
            pltpu.VMEM((2, trailing.shape[0], width), jnp.float32),
            pltpu.SemaphoreType.DMA((2 * steps, fanout)),
            pltpu.SemaphoreType.DMA((2 * steps, fanout, 4)),
            pltpu.SemaphoreType.DMA((2 * fanout,)),
            pltpu.SemaphoreType.DMA((trailing.shape[1] // block,)),
        ],
        compiler_params=pltpu.CompilerParams(
            collective_id=0, has_side_effects=True, vmem_limit_bytes=60 * 1024 * 1024
        ),
        name="spread_multiply",
    )(idx, factor_a, factor_b, trailing)


def contract_rows(former, latter):
    return lax.dot_general(
        former, latter, (((0,), (0,)), ((), ())), preferred_element_type=jnp.float32
    )


def on_device(
    trailing, rows_a, counts_a, factor_a, rows_b, counts_b, factor_b, factor_top, base_a, base_b
):
    row_count = lax.axis_size("row")
    col_count = lax.axis_size("col")
    fanout = row_count // col_count
    row_index = lax.axis_index("row")
    col_index = lax.axis_index("col")
    slots = rows_a.shape[1]
    total_rows, width = factor_a.shape
    block = total_rows // slots
    row_blocks = trailing.shape[0] // block
    part_width = width // col_count
    width_start = col_index * part_width
    slot_ids = jnp.arange(slots, dtype=jnp.int32)

    def own(table):
        return lax.dynamic_index_in_dim(table, row_index, 0, keepdims=False)

    live_a = slot_ids < own(counts_a)
    live_b = slot_ids < own(counts_b)
    own_a, own_b = own(rows_a), own(rows_b)
    blocks = jnp.arange(row_blocks, dtype=jnp.int32)
    gate_a = jnp.any((own_a[None, :] == blocks[:, None]) & live_a[None, :], axis=1)
    gate_b = jnp.any((own_b[None, :] == blocks[:, None]) & live_b[None, :], axis=1)

    def masked(factor, live):
        return jnp.where(
            live[:, None, None], factor.reshape(slots, block, width), 0
        ).reshape(total_rows, width).astype(factor.dtype)

    parts = jnp.arange(fanout, dtype=jnp.int32)
    owners = col_index + parts * col_count
    idx = jnp.stack(
        [jnp.take(rows, owners, axis=0) * fanout + parts[:, None] for rows in (rows_a, rows_b)]
    ).astype(jnp.int32)
    part = spread_multiply(
        idx, masked(factor_a, live_a), masked(factor_b, live_b), trailing, row_count, col_count
    )
    reduced = lax.psum_scatter(part, "col", scatter_dimension=2, tiled=True).astype(jnp.float32)

    def gated(value, gate):
        return jnp.where(
            gate[:, None, None], value.reshape(row_blocks, block, -1), 0
        ).reshape(row_blocks * block, -1)

    def by_slot(value, own_rows, live):
        picked = jnp.take(value.reshape(row_blocks, block, -1), own_rows, axis=0)
        return jnp.where(live[:, None, None], picked, 0).reshape(total_rows, -1)

    col_a = gated(-reduced[0], gate_a).astype(jnp.bfloat16)
    whole_a = lax.all_gather(col_a, "col", axis=1, tiled=True)
    column_a = by_slot(whole_a, own_a, live_a)
    top_part = lax.dynamic_slice_in_dim(factor_top, width_start, part_width, 1)
    cross = jnp.dot(whole_a, top_part, preferred_element_type=jnp.float32)
    col_b = gated(-(reduced[1] + cross), gate_b).astype(jnp.bfloat16)
    column_b = by_slot(
        lax.all_gather(col_b, "col", axis=1, tiled=True), own_b, live_b
    )
    sums = lax.psum(
        (
            contract_rows(by_slot(col_a, own_a, live_a), factor_a),
            contract_rows(by_slot(col_a, own_b, live_b), factor_b),
            contract_rows(by_slot(col_b, own_b, live_b), factor_b),
        ),
        "row",
    )
    diag_a = base_a - sums[0]
    top_b = (
        -(
            sums[1]
            + jnp.dot(diag_a, factor_top.astype(jnp.float32), precision=lax.Precision.HIGHEST)
        )
    ).astype(jnp.bfloat16)
    top_whole = lax.all_gather(top_b, "col", axis=0, tiled=True)
    top_cols = lax.dynamic_slice_in_dim(top_whole, width_start, part_width, 1)
    diag_b = base_b - sums[2] - contract_rows(top_cols, factor_top)
    return (column_a, diag_a, column_b, top_b, diag_b)


def solution(mesh):
    in_specs = (
        P("row", "col"),
        P(),
        P(),
        P("row", None),
        P(),
        P(),
        P("row", None),
        P(),
        P("col", None),
        P("col", None),
    )
    out_specs = (P("row", None), P("col", None), P("row", None), P("col", None), P("col", None))
    return jax.shard_map(
        on_device, mesh=mesh, in_specs=in_specs, out_specs=out_specs, check_vma=False
    )
```

```python
import jax
import jax.numpy as jnp
from jax import lax
from jax.sharding import PartitionSpec as P


def contract_rows(former, latter):
    return lax.dot_general(
        former, latter, (((0,), (0,)), ((), ())), preferred_element_type=jnp.float32
    )


def on_device(
    trailing, rows_a, counts_a, factor_a, rows_b, counts_b, factor_b, factor_top, base_a, base_b
):
    row_count = lax.axis_size("row")
    col_count = lax.axis_size("col")
    fanout = row_count // col_count
    row_index = lax.axis_index("row")
    col_index = lax.axis_index("col")
    slots = rows_a.shape[1]
    total_rows, width = factor_a.shape
    block = total_rows // slots
    row_blocks = trailing.shape[0] // block
    part_width = width // col_count
    width_start = col_index * part_width
    slot_ids = jnp.arange(slots, dtype=jnp.int32)

    def own(table):
        return lax.dynamic_index_in_dim(table, row_index, 0, keepdims=False)

    live_a = slot_ids < own(counts_a)
    live_b = slot_ids < own(counts_b)
    own_a, own_b = own(rows_a), own(rows_b)
    blocks = jnp.arange(row_blocks, dtype=jnp.int32)
    gate_a = jnp.any((own_a[None, :] == blocks[:, None]) & live_a[None, :], axis=1)
    gate_b = jnp.any((own_b[None, :] == blocks[:, None]) & live_b[None, :], axis=1)

    pieces = jnp.stack([factor_a, factor_b]).reshape(
        2, row_count, total_rows // row_count, width
    )
    arrived = []
    for shift in range(row_count):
        piece = lax.dynamic_index_in_dim(
            pieces, (row_index + shift) % row_count, 1, keepdims=False
        )
        if shift:
            pairs = [
                (
                    owner * col_count + owner % col_count,
                    (owner + shift) % row_count * col_count + owner % col_count,
                )
                for owner in range(row_count)
            ]
            piece = lax.ppermute(piece, ("row", "col"), pairs)
        arrived.append(piece)
    arrived = jnp.stack(arrived)
    mine = jnp.stack(
        [
            lax.dynamic_index_in_dim(
                arrived,
                (row_index - col_index - part * col_count) % row_count,
                0,
                keepdims=False,
            )
            for part in range(fanout)
        ],
        axis=1,
    )
    held = lax.all_gather(mine, "row", axis=2, tiled=True)
    owners = col_index + jnp.arange(fanout, dtype=jnp.int32) * col_count

    def partial_product(node, rows, counts):
        own_rows = jnp.take(rows, owners, axis=0)
        live = slot_ids[None, :] < jnp.take(counts, owners, axis=0)[:, None]
        match = (own_rows[None, :, :] == blocks[:, None, None]) & live[None, :, :]
        filled = jnp.any(match, axis=2).reshape(-1)
        source = jnp.argmax(match, axis=2).astype(jnp.int32)
        source = (source + jnp.arange(fanout, dtype=jnp.int32) * slots).reshape(-1)
        picked = jnp.take(held[node].reshape(fanout * slots, block, width), source, axis=0)
        spread = jnp.where(filled[:, None, None], picked, 0).reshape(-1, width)
        return jnp.dot(trailing, spread, preferred_element_type=jnp.float32).astype(
            jnp.bfloat16
        )

    part = jnp.stack(
        [partial_product(0, rows_a, counts_a), partial_product(1, rows_b, counts_b)]
    )
    reduced = lax.psum_scatter(part, "col", scatter_dimension=2, tiled=True).astype(jnp.float32)

    def gated(value, gate):
        return jnp.where(
            gate[:, None, None], value.reshape(row_blocks, block, -1), 0
        ).reshape(row_blocks * block, -1)

    def by_slot(value, own_rows, live):
        picked = jnp.take(value.reshape(row_blocks, block, -1), own_rows, axis=0)
        return jnp.where(live[:, None, None], picked, 0).reshape(total_rows, -1)

    col_a = gated(-reduced[0], gate_a).astype(jnp.bfloat16)
    whole_a = lax.all_gather(col_a, "col", axis=1, tiled=True)
    column_a = by_slot(whole_a, own_a, live_a)
    top_part = lax.dynamic_slice_in_dim(factor_top, width_start, part_width, 1)
    cross = jnp.dot(whole_a, top_part, preferred_element_type=jnp.float32)
    col_b = gated(-(reduced[1] + cross), gate_b).astype(jnp.bfloat16)
    column_b = by_slot(
        lax.all_gather(col_b, "col", axis=1, tiled=True), own_b, live_b
    )
    sums = lax.psum(
        (
            contract_rows(by_slot(col_a, own_a, live_a), factor_a),
            contract_rows(by_slot(col_a, own_b, live_b), factor_b),
            contract_rows(by_slot(col_b, own_b, live_b), factor_b),
        ),
        "row",
    )
    diag_a = base_a - sums[0]
    top_b = (
        -(
            sums[1]
            + jnp.dot(diag_a, factor_top.astype(jnp.float32), precision=lax.Precision.HIGHEST)
        )
    ).astype(jnp.bfloat16)
    top_whole = lax.all_gather(top_b, "col", axis=0, tiled=True)
    top_cols = lax.dynamic_slice_in_dim(top_whole, width_start, part_width, 1)
    diag_b = base_b - sums[2] - contract_rows(top_cols, factor_top)
    return (column_a, diag_a, column_b, top_b, diag_b)


def solution(mesh):
    in_specs = (
        P("row", "col"),
        P(),
        P(),
        P("row", None),
        P(),
        P(),
        P("row", None),
        P(),
        P("col", None),
        P("col", None),
    )
    out_specs = (P("row", None), P("col", None), P("row", None), P("col", None), P("col", None))
    return jax.shard_map(
        on_device, mesh=mesh, in_specs=in_specs, out_specs=out_specs, check_vma=False
    )
```
